32 devices in a mesh: groups: 1, ctx: 16 (over z, y, x), tp: 1, dp: 2 (over core).
Axes of the slice: x: 2, y: 2, z: 4, core: 2. Of those that a mesh axis runs over, the one named last changes fastest.
Arguments:
- queries: bfloat16 [16384, 4096], P(('groups', 'ctx', 'dp'), 'tp'), may hold values from -128 to 128
- keys: bfloat16 [16384, 512], P(('groups', 'ctx', 'dp'), 'tp'), may hold values from -12 to 12
- values: bfloat16 [16384, 512], P(('groups', 'ctx', 'dp'), 'tp'), may hold values from -8 to 8
- doc_ids: int32 [16384], P(('groups', 'ctx', 'dp')), may hold values from 0 to 63, never falling along the last dimension, each value on 1 to 2048 neighbouring positions
- clip_limits: int32 [4096], P('tp'), may hold values from 256 to 2048
- out_weight: bfloat16 [4096, 8192], P('tp', ('ctx', 'dp')), may hold values from -0.09375 to 0.09375
Outputs:
- attended: bfloat16 [16384, 8192], P(('groups', 'ctx', 'dp'), 'tp')
The draws below stay inside these ranges and needn't reach their ends.
Inputs may be any that keep to these rules, and one draw needn't show every extreme that they name: `doc_ids`: document numbers never fall along the window; every document holds at most 2048 tokens, and one holds exactly 2048.
All inputs are finite; a program needn't handle non-finite values.
Results may differ from the reference program's by a relative error of at most 0.0095.
Values may be sent and summed in bfloat16 or wider, within the bound.
No kernel may reach another device: no remote copies, remote signals or barrier semaphores. Data moves between devices by JAX's collectives and lax.ppermute only.
A program may use at most 384 MiB of HBM per device.

```python
import math
import jax
import jax.numpy as jnp
import numpy as np
from jax import lax

D = 8192
H = 32
KVH = 4
HD = 128
TOK_DEV = 512
REACH = 4
PACKED_SPAN = 16384
DOC_MOST = 2048
DOCS = 64
N_TP = 1


def drawn_pair(key):
    seed_keys = jax.random.fold_in(key, 101)
    seed_queries = jax.random.fold_in(key, 202)
    per_group = H // KVH
    key_sample = jax.random.normal(seed_keys, (PACKED_SPAN, KVH, HD), jnp.float32)
    query_draw = jax.random.normal(seed_queries, (PACKED_SPAN, KVH, per_group, HD), jnp.float32)
    query_draw = jnp.clip(query_draw, -6.0, 6.0)
    key_sample = jnp.clip(key_sample, -6.0, 6.0)
    return (query_draw.reshape(PACKED_SPAN, H * HD), key_sample.reshape(PACKED_SPAN, KVH * HD))


def draw_queries(key, part):
    return drawn_pair(key)[0].astype(jnp.bfloat16)


def draw_keys(key, part):
    return drawn_pair(key)[1].astype(jnp.bfloat16)


def with_ends(entries, key, smallest, largest):
    longest = entries.shape.index(max(entries.shape))
    spots = []
    for shift in (0, 1):
        where = [jax.random.randint(jax.random.fold_in(key, axis), (), 0, length) for axis, length in enumerate(entries.shape)]
        where[longest] = (where[longest] + shift) % entries.shape[longest]
        spots.append(tuple(where))
    return entries.at[spots[0]].set(smallest).at[spots[1]].set(largest)


def level_of(rng, extent, cuts, smallest, top_value):
    factor_of = 1.0
    for axis_at, parts in cuts:
        draws = jax.random.uniform(jax.random.fold_in(jax.random.fold_in(rng, 6), axis_at), (parts,), jnp.float32, smallest / len(cuts), top_value / len(cuts))
        factor_of = factor_of * jnp.repeat(jnp.exp(draws), extent[axis_at] // parts).reshape((-1,) + (1,) * (len(extent) - 1 - axis_at))
    return factor_of


def split_up(amount, total, most, lean):
    loads = [(1 << 20) // math.isqrt(standing ** lean) + 1 for standing in range(2, amount + 1)]
    spare, counts = total - most - (amount - 1), [1] * (amount - 1)
    while spare > 0:
        free = [i for i in range(amount - 1) if counts[i] < most]
        mass, remaining = sum([loads[i] for i in free]), spare
        for i in free:
            addition = min(most - counts[i], max(1, remaining * loads[i] // mass), spare)
            counts[i] = counts[i] + addition
            spare = spare - addition
    return np.array([most] + counts)


def ragged_sizes(own_key, amount, total, bound, lean):
    if amount == 2:
        one = jax.random.randint(own_key, (), max(1, total - bound), min(bound, total - 1) + 1)
        return jnp.stack([one, total - one])
    lengths = jnp.asarray(split_up(amount, total, bound, lean), jnp.int32)
    twos = (amount - 1) // 2
    source_of, sink = lengths[1:1 + 2 * twos:2], lengths[2:2 + 2 * twos:2]
    slack = jnp.minimum(source_of - 1, bound - sink)
    passed = jax.random.randint(jax.random.fold_in(own_key, 1), (twos,), 0, 1 << 20) % (slack + 1)
    lengths = lengths.at[1:1 + 2 * twos:2].set(source_of - passed).at[2:2 + 2 * twos:2].set(sink + passed)
    return lengths[jax.random.permutation(jax.random.fold_in(own_key, 2), amount)]


def bell_draw(own_key, shape, deviation, limit, pieces=(), kind=jnp.bfloat16):
    result = jax.random.normal(own_key, shape, jnp.float32) * deviation
    if len(pieces) > 0:
        result = level_of(own_key, shape, pieces, -0.22, 0.18) * result
    return jnp.clip(result, min=-limit, max=limit).astype(kind)


def setup_inputs(seed: int = 0, part: int = 0) -> dict:
    splits = jax.random.split(jax.random.key(seed), 7)
    part_splits = jax.random.split(jax.random.fold_in(splits[6], part), 7)
    queries = draw_queries(jax.random.fold_in(jax.random.fold_in(splits[6], part), 71), part)
    keys = draw_keys(jax.random.fold_in(jax.random.fold_in(splits[6], part), 71), part)
    values = bell_draw(part_splits[2], (PACKED_SPAN, KVH * HD), 2.0, 8.0, ((0, 32),))
    doc_ids = jnp.searchsorted(jnp.cumsum(ragged_sizes(part_splits[3], DOCS, PACKED_SPAN, DOC_MOST, 2)), jnp.arange(PACKED_SPAN), side="right").astype(jnp.int32)
    clip_limits = with_ends(jax.random.randint(splits[4], (H * HD,), 256, 2049), jax.random.fold_in(splits[4], 1), 256, 2048).astype(jnp.int32)
    out_weight = bell_draw(splits[5], (H * HD, D), (H * HD) ** -0.5, 0.09375, ((1, 32),))
    return {"queries": queries, "keys": keys, "values": values, "doc_ids": doc_ids, "clip_limits": clip_limits, "out_weight": out_weight}


neg_big = -1e30
unit_scale = 1024.0


def reference(queries, keys, values, doc_ids, clip_limits, out_weight):
    per_group = H // KVH
    pad_rows = REACH * TOK_DEV
    span_rows = pad_rows + TOK_DEV
    keys_pad = jnp.concatenate([jnp.zeros((pad_rows, KVH * HD), keys.dtype), keys], 0).reshape(pad_rows + PACKED_SPAN, KVH, HD)
    values_pad = jnp.concatenate([jnp.zeros((pad_rows, KVH * HD), values.dtype), values], 0).reshape(pad_rows + PACKED_SPAN, KVH, HD)
    doc_list = doc_ids.astype(jnp.int32)
    docs_pad = jnp.concatenate([jnp.full((pad_rows,), -1, jnp.int32), doc_list], 0)
    inv_root = 1.0 / (HD ** 0.5)

    def one_block(block_id):
        first = (block_id * TOK_DEV).astype(jnp.int32)
        q_block = lax.dynamic_slice_in_dim(queries, first, TOK_DEV, 0).reshape(TOK_DEV, KVH, per_group, HD).astype(jnp.float32)
        k_block = lax.dynamic_slice_in_dim(keys_pad, first, span_rows, 0).astype(jnp.float32)
        v_block = lax.dynamic_slice_in_dim(values_pad, first, span_rows, 0).astype(jnp.float32)
        key_doc = lax.dynamic_slice_in_dim(docs_pad, first, span_rows, 0)
        query_doc = lax.dynamic_slice_in_dim(doc_list, first, TOK_DEV, 0)
        query_pos = first + jnp.arange(TOK_DEV, dtype=jnp.int32)
        key_location = first - pad_rows + jnp.arange(span_rows, dtype=jnp.int32)
        visible = (key_doc[None, :] == query_doc[:, None]) & (key_location[None, :] <= query_pos[:, None]) & (key_location[None, :] >= 0)
        scores = jnp.einsum('tkge,jke->kgtj', q_block, k_block) * inv_root
        scores = jnp.where(visible, scores, neg_big)
        row_max = jnp.max(scores, axis=-1, keepdims=True)
        powers = jnp.where(visible, jnp.exp(scores - row_max), 0.0)
        row_total = jnp.sum(powers, axis=-1)
        weights = lax.optimization_barrier(powers.astype(jnp.bfloat16)).astype(jnp.float32)
        mixed = jnp.einsum('kgtj,jke->tkge', weights, v_block)
        return mixed / jnp.transpose(row_total, (2, 0, 1))[..., None]

    context = lax.map(one_block, jnp.arange(PACKED_SPAN // TOK_DEV, dtype=jnp.int32)).reshape(PACKED_SPAN, H * HD)
    bounds = clip_limits.astype(jnp.float32) / unit_scale
    clipped = jnp.clip(context, -bounds, bounds).astype(jnp.bfloat16)
    chan_dev = H * HD // N_TP
    summed = jnp.zeros((PACKED_SPAN, D), jnp.float32)
    for tp_part in range(N_TP):
        partial_value = jnp.dot(clipped[:, tp_part * chan_dev:(tp_part + 1) * chan_dev], out_weight[tp_part * chan_dev:(tp_part + 1) * chan_dev], preferred_element_type=jnp.float32).astype(jnp.bfloat16)
        summed = summed + partial_value.astype(jnp.float32)
    return summed.astype(jnp.bfloat16)
```

```python
import functools

import jax
import jax.numpy as jnp
from jax import lax
from jax.experimental import pallas as pl
from jax.experimental.pallas import tpu as pltpu
from jax.sharding import PartitionSpec as P


HD = 128
Q_TILE = 256
K_TILE = 512
neg_big = -1e30
unit_scale = 1024.0
LOG2E = 1.4426950408889634


def attend_kernel(
    bounds_ref, q_ref, start_ref, clip_ref, *refs, heads, tok, q_tile, k_tile
):
    shards = refs[:12]
    o_ref, k_scr, v_scr, m_scr, a_scr = refs[12:]
    qi = pl.program_id(1)
    own_side = bounds_ref[0]

    @pl.when((qi == 0) & (pl.program_id(0) == 0))
    def _():
        v_scr[:, :, HD:] = jnp.ones((6, tok, HD), jnp.bfloat16)

    @pl.when(qi == 0)
    def _():
        for spot in range(6):
            k_scr[spot] = shards[2 * spot][:tok]
            v_scr[spot, :, :HD] = shards[2 * spot + 1][:tok]

    scale = LOG2E / HD**0.5
    q_first = (4 + own_side) * tok + qi * q_tile
    per_shard = tok // k_tile
    last = q_first // k_tile
    first = bounds_ref[1 + qi]
    m_scr[...] = jnp.full_like(m_scr, neg_big)
    a_scr[...] = jnp.zeros_like(a_scr)
    start_col = start_ref[...]
    row_pos = q_first + lax.broadcasted_iota(jnp.int32, (q_tile, k_tile), 0)

    def step(i, carry):
        blk = last - i
        shard = blk // per_shard
        spot = lax.rem(shard + own_side, 2) * 3 + shard // 2
        rows = pl.ds(pl.multiple_of(lax.rem(blk, per_shard) * k_tile, k_tile), k_tile)
        k_blk = k_scr[spot, rows]
        v_blk = v_scr[spot, rows]
        key_pos = blk * k_tile + lax.broadcasted_iota(
            jnp.int32, (q_tile, k_tile), 1
        )
        seen = (key_pos >= start_col) & (key_pos <= row_pos)
        bias = jnp.where(seen, 0.0, neg_big)
        for h in range(heads):
            s = lax.dot_general(
                q_ref[:, h * HD : (h + 1) * HD],
                k_blk,
                (((1,), (1,)), ((), ())),
                preferred_element_type=jnp.float32,
            )
            s = s + bias
            m_old = m_scr[h]
            m_new = jnp.maximum(m_old, jnp.max(s, axis=-1, keepdims=True))
            m_scr[h] = m_new
            wide = jnp.concatenate([m_new] * (k_tile // HD), axis=1)
            p = jnp.exp2((s - wide) * scale).astype(jnp.bfloat16)
            alpha = jnp.exp2((m_old - m_new) * scale)
            a_scr[h] = a_scr[h] * jnp.concatenate([alpha, alpha], axis=1) + jnp.dot(
                p, v_blk, preferred_element_type=jnp.float32
            )
        return carry

    lax.fori_loop(0, last - first + 1, step, 0)
    for h in range(heads):
        ctx = a_scr[h, :, :HD] / a_scr[h, :, HD:]
        lim = clip_ref[:, h * HD : (h + 1) * HD].astype(jnp.float32) / unit_scale
        ctx = jnp.minimum(jnp.maximum(ctx, -lim), lim)
        o_ref[:, h * HD : (h + 1) * HD] = ctx.astype(o_ref.dtype)


def attend(bounds, queries, start, limits, shards, g0, groups, kv_heads):
    tok = queries.shape[0]
    heads = queries.shape[1] // HD // kv_heads
    q_tile, k_tile = min(Q_TILE, tok), min(K_TILE, tok)
    width = heads * HD
    shard_specs, shard_args = [], []
    for a in shards:
        rows = a.shape[0]
        shard_args += [a, a]
        shard_specs += [
            pl.BlockSpec((rows, HD), lambda g, i, *_: (0, g0 + g)),
            pl.BlockSpec((rows, HD), lambda g, i, *_: (0, kv_heads + g0 + g)),
        ]
    return pl.pallas_call(
        functools.partial(
            attend_kernel, heads=heads, tok=tok, q_tile=q_tile, k_tile=k_tile
        ),
        out_shape=jax.ShapeDtypeStruct((tok, groups * width), jnp.bfloat16),
        grid_spec=pltpu.PrefetchScalarGridSpec(
            num_scalar_prefetch=1,
            grid=(groups, tok // q_tile),
            in_specs=[
                pl.BlockSpec((q_tile, width), lambda g, i, *_: (i, g0 + g)),
                pl.BlockSpec((q_tile, 1), lambda g, i, *_: (i, 0)),
                pl.BlockSpec((1, width), lambda g, i, *_: (0, g0 + g)),
            ]
            + shard_specs,
            out_specs=pl.BlockSpec((q_tile, width), lambda g, i, *_: (i, g)),
            scratch_shapes=[
                pltpu.VMEM((6, tok, HD), jnp.bfloat16),
                pltpu.VMEM((6, tok, 2 * HD), jnp.bfloat16),
                pltpu.VMEM((heads, q_tile, HD), jnp.float32),
                pltpu.VMEM((heads, q_tile, 2 * HD), jnp.float32),
            ],
        ),
        compiler_params=pltpu.CompilerParams(vmem_limit_bytes=40 << 20),
        cost_estimate=pl.CostEstimate(
            flops=4 * tok * width * groups * 4 * tok,
            transcendentals=tok * heads * groups * 4 * tok,
            bytes_accessed=4 * tok * width * groups,
        ),
    )(bounds, queries, start, limits, *shard_args)


def project_kernel(idx_ref, *refs, n_ctx, layout, aliased, tok, cols):
    own = refs[:n_ctx]
    partner = refs[n_ctx : 2 * n_ctx]
    n_pieces = sum(len(p) for p in layout)
    pieces = refs[2 * n_ctx : 2 * n_ctx + n_pieces]
    rest = refs[2 * n_ctx + n_pieces + (1 if aliased else 0) :]
    out_ref, send_ref, c_buf, w_buf, o_buf, c_sem, w_sem, o_sem = rest
    width = own[0].shape[1]
    ctx_copies = []
    for side, group in enumerate((own, partner)):
        for g, ref in enumerate(group):
            ctx_copies.append(
                pltpu.make_async_copy(
                    ref,
                    c_buf.at[side, :, pl.ds(g * width, width)],
                    c_sem.at[side * n_ctx + g],
                )
            )
    weight_copies = []
    at = 0
    for s, plan in enumerate(layout):
        mine = []
        for src, row, rows in plan:
            ref = pieces[at] if src is None else pieces[at].at[src]
            mine.append(
                pltpu.make_async_copy(
                    ref, w_buf.at[s, pl.ds(row, rows)], w_sem.at[at]
                )
            )
            at += 1
        weight_copies.append(mine)
    for cp in ctx_copies[:n_ctx] + weight_copies[0]:
        cp.start()
    for cp in ctx_copies[n_ctx:]:
        cp.start()
    for mine in weight_copies[1:]:
        for cp in mine:
            cp.start()
    out_copies = []
    for s in range(len(layout)):
        if s == 0:
            for cp in ctx_copies:
                cp.wait()
        for cp in weight_copies[s]:
            cp.wait()

        @pl.loop(0, 2)
        def _(side):
            o_buf[s, side] = jnp.dot(
                c_buf[side], w_buf[s], preferred_element_type=jnp.float32
            ).astype(jnp.bfloat16)

        spot = pl.multiple_of(idx_ref[s] * cols, cols)
        for side, dst in enumerate(
            (out_ref.at[:, pl.ds(spot, cols)], send_ref.at[:, pl.ds(s * cols, cols)])
        ):
            cp = pltpu.make_async_copy(
                o_buf.at[s, side], dst, o_sem.at[2 * s + side]
            )
            cp.start()
            out_copies.append(cp)
    for cp in out_copies:
        cp.wait()


def project(idx, own, partner, layout, pieces, out, out_cols, cols):
    tok = own[0].shape[0]
    depth = own[0].shape[1] * len(own)
    n = len(layout)
    aliased = out is not None
    args = [idx, *own, *partner, *pieces] + ([out] if aliased else [])
    hbm = pl.BlockSpec(memory_space=pl.ANY)
    return pl.pallas_call(
        functools.partial(
            project_kernel,
            n_ctx=len(own),
            layout=layout,
            aliased=aliased,
            tok=tok,
            cols=cols,
        ),
        out_shape=(
            jax.ShapeDtypeStruct((tok, out_cols), jnp.bfloat16),
            jax.ShapeDtypeStruct((tok, n * cols), jnp.bfloat16),
        ),
        grid_spec=pltpu.PrefetchScalarGridSpec(
            num_scalar_prefetch=1,
            grid=(1,),
            in_specs=[hbm] * (len(args) - 1),
            out_specs=(hbm, hbm),
            scratch_shapes=[
                pltpu.VMEM((2, tok, depth), jnp.bfloat16),
                pltpu.VMEM((n, depth, cols), jnp.bfloat16),
                pltpu.VMEM((n, 2, tok, cols), jnp.bfloat16),
                pltpu.SemaphoreType.DMA((2 * len(own),)),
                pltpu.SemaphoreType.DMA((len(pieces),)),
                pltpu.SemaphoreType.DMA((2 * n,)),
            ],
        ),
        input_output_aliases={len(args) - 1: 0} if aliased else {},
        compiler_params=pltpu.CompilerParams(vmem_limit_bytes=48 << 20),
        cost_estimate=pl.CostEstimate(
            flops=4 * tok * depth * n * cols,
            transcendentals=0,
            bytes_accessed=2 * depth * (2 * tok + n * cols),
        ),
    )(*args)


def place_kernel(idx_ref, *refs, n_src, per, cols):
    srcs = refs[:n_src]
    out_ref, sem = refs[n_src + 1 :]
    copies = []
    for a in range(n_src):
        for s in range(per[a]):
            at = len(copies)
            spot = pl.multiple_of(idx_ref[at] * cols, cols)
            cp = pltpu.make_async_copy(
                srcs[a].at[:, pl.ds(s * cols, cols)],
                out_ref.at[:, pl.ds(spot, cols)],
                sem.at[at],
            )
            cp.start()
            copies.append(cp)
    for cp in copies:
        cp.wait()


def place(idx, srcs, out, cols):
    per = tuple(a.shape[1] // cols for a in srcs)
    hbm = pl.BlockSpec(memory_space=pl.ANY)
    return pl.pallas_call(
        functools.partial(place_kernel, n_src=len(srcs), per=per, cols=cols),
        out_shape=jax.ShapeDtypeStruct(out.shape, out.dtype),
        grid_spec=pltpu.PrefetchScalarGridSpec(
            num_scalar_prefetch=1,
            grid=(1,),
            in_specs=[
                pl.BlockSpec(a.shape, lambda i, *_: (0, 0)) for a in srcs
            ]
            + [hbm],
            out_specs=hbm,
            scratch_shapes=[pltpu.SemaphoreType.DMA((sum(per),))],
        ),
        input_output_aliases={len(srcs) + 1: 0},
    )(idx, *srcs, out)


def steps(queries, keys, values, doc_ids, clip_limits, out_weight):
    tok = queries.shape[0]
    kv_heads = keys.shape[1] // HD
    kv_cols = 2 * keys.shape[1]
    depth, cols = out_weight.shape
    n_ctx, n_dp = lax.axis_size("ctx"), lax.axis_size("dp")
    out_cols = cols * n_ctx * n_dp
    c, d = lax.axis_index("ctx"), lax.axis_index("dp")
    layers = n_ctx // 4

    def swap(a):
        return lax.ppermute(a, "dp", [(0, 1), (1, 0)])

    def lift(a):
        pairs = [(i, i + 4) for i in range(n_ctx - 4) if i % 4 >= 2]
        return lax.ppermute(a, "ctx", pairs)

    def flip(a, bit):
        return lax.ppermute(a, "ctx", [(i, i ^ bit) for i in range(n_ctx)])

    def rise(a, by):
        return lax.ppermute(
            a, "ctx", [(i, (i + by) % n_ctx) for i in range(n_ctx)]
        )

    doc_rows = jnp.pad(doc_ids.astype(jnp.bfloat16), (0, 16 * kv_cols - tok))
    bundle = jnp.concatenate(
        [
            jnp.concatenate([keys, values], axis=1),
            doc_rows.reshape(16, kv_cols),
        ],
        axis=0,
    )
    below = lift(bundle)
    place_in_layer = lax.rem(c, 4)
    before_2 = flip(jnp.where(place_in_layer >= 2, below, bundle), 2)
    before_1 = flip(jnp.where(place_in_layer % 2 == 1, before_2, bundle), 1)
    mine = (before_2, before_1, bundle)
    theirs = (swap(before_2), swap(before_1), swap(bundle))
    shards = [pltpu.with_memory_space_constraint(a, pltpu.HBM) for a in mine + theirs]

    w = {(0, 0): out_weight}
    w[1, 0] = rise(out_weight, 4)
    w[3, 0] = rise(out_weight, -4)
    w[0, 1] = flip(out_weight, 1)
    w[0, 2] = flip(out_weight, 2)
    w[0, 3] = flip(w[0, 2], 1)
    w[2, 0] = rise(w[1, 0], 4)
    w[1, 1] = flip(w[1, 0], 1)
    w[1, 2] = flip(w[1, 0], 2)
    w[2, 1] = flip(w[2, 0], 1)
    w[2, 2] = flip(w[2, 0], 2)
    w[3, 1] = flip(w[3, 0], 1)
    w[3, 2] = flip(w[3, 0], 2)
    w[1, 3] = rise(w[0, 3], 4)
    w[2, 3] = rise(w[1, 3], 4)
    w[3, 3] = flip(w[3, 1], 2)

    def docs_of(a, valid):
        ids = a[tok:].reshape(-1)[:tok].astype(jnp.int32)
        return jnp.where(valid, ids, -1)

    window_docs = jnp.concatenate(
        [
            docs_of(a, c >= age)
            for side in (mine, theirs)
            for age, a in zip((2, 1, 0), side)
        ]
    )
    start = jnp.sum(
        (window_docs[None, :] < doc_ids[:, None]).astype(jnp.int32),
        axis=1,
        keepdims=True,
    )
    q_tile, k_tile = min(Q_TILE, tok), min(K_TILE, tok)
    bounds = jnp.concatenate(
        [d[None].astype(jnp.int32), start[::q_tile, 0] // k_tile]
    )
    limits = clip_limits.reshape(1, -1)

    groups = 1
    own, partner = [], []
    for g0 in range(0, kv_heads, groups):
        own.append(
            attend(
                bounds, queries, start, limits, shards, g0, groups, kv_heads
            )
        )
        partner.append(swap(own[-1]))

    def columns_of(shards, side):
        spots = [
            (lax.rem(c // 4 - layer + layers, layers) * 4 + (lax.rem(c, 4) ^ f)) * n_dp
            + side
            for layer, f in shards
        ]
        return jnp.stack(spots).astype(jnp.int32)

    def placed(out, first, last):
        shards = [s for part in PARTS[first:last] for s in part]
        return place(columns_of(shards, 1 - d), arrived[first:last], out, cols)

    out = None
    arrived = []
    for n, part in enumerate(PARTS):
        if n == len(PARTS) - 1:
            out = placed(out, 0, n)
        out, sent = project(
            columns_of(part, d),
            own,
            partner,
            tuple(((None, 0, depth),) for _ in part),
            [w[s] for s in part],
            out,
            out_cols,
            cols,
        )
        arrived.append(swap(sent))
    out = placed(out, len(PARTS) - 1, len(PARTS))
    if lax.axis_size("tp") > 1:
        out = lax.psum_scatter(out, "tp", scatter_dimension=1, tiled=True)
    return out


PARTS = (
    ((0, 0), (0, 1), (0, 2), (0, 3)),
    ((1, 0), (1, 1), (1, 2)),
    ((3, 0), (3, 1), (3, 2)),
    ((2, 0), (1, 3), (2, 2)),
    ((2, 1), (2, 3)),
    ((3, 3),),
)


def solution(mesh):
    placed = (
        P(("groups", "ctx", "dp"), "tp"),
        P(("groups", "ctx", "dp"), "tp"),
        P(("groups", "ctx", "dp"), "tp"),
        P(("groups", "ctx", "dp")),
        P("tp"),
        P("tp", ("ctx", "dp")),
    )
    return jax.shard_map(
        steps,
        mesh=mesh,
        in_specs=placed,
        out_specs=P(("groups", "ctx", "dp"), "tp"),
        check_vma=False,
    )
```
